256 devices in a mesh: band: 4 (over x_lo, core), grid: 64 (over z, x_hi, y).
Axes of the slice: x: 4 (x_hi: 2, x_lo: 2; x = x_hi * 2 + x_lo), y: 4, z: 8, core: 2. Of those that a mesh axis runs over, the one named last changes fastest.
Arguments:
- states: float32 [64, 512, 8, 128], P('band', 'grid'), may hold values from -6 to 6
- potential: float32 [512, 8, 128], P('grid'), may hold values from -1 to 1
- proj_index: int32 [128, 128], replicated, may hold values from 0 to 524287, as said below
- proj_value: float32 [128, 128], replicated, may hold values from 0 to 1
- proj_strength: float32 [128], replicated, may hold values from 0.5 to 4
Outputs:
- filtered: float32 [64, 512, 8, 128], P('band', 'grid')
- gram: float32 [64, 64], P('band')
- hamiltonian: float32 [64, 64], P('band')
The draws below stay inside these ranges and needn't reach their ends.
Inputs may be any that keep to these rules, and one draw needn't show every extreme that they name: `proj_index`: along the first grid dimension every support point lies within 8 planes of its atom's centre plane.
All inputs are finite; a program needn't handle non-finite values.
Results may differ from the reference program's by a relative error of at most 0.0001.
Values sent between devices are 32-bit elements; how exact they have to be, the bound alone decides.
No kernel may reach another device: no remote copies, remote signals or barrier semaphores. Data moves between devices by JAX's collectives and lax.ppermute only.
A program may use at most 64 MiB of HBM per device.

```python
import math
import jax
import jax.numpy as jnp
from jax import lax

PL = 8
NY = 8
NZ = 128
RADIUS = 4
DEGREE = 4
NPTS = 128
NATOMS = 128
NX = 512
NPOINTS = 524288
NSTATES = 64


def support_geometry(key):
    subkeys = jax.random.split(jax.random.fold_in(key, 17), 7)
    centre_x = jax.random.randint(subkeys[0], (NATOMS, 1), 0, NX)
    centre_y = jax.random.randint(subkeys[1], (NATOMS, 1), 0, NY)
    centre_z = jax.random.randint(subkeys[2], (NATOMS, 1), 0, NZ)
    offset_x = jax.random.randint(subkeys[3], (NATOMS, NPTS), -PL, PL + 1)
    offset_y = jax.random.randint(subkeys[4], (NATOMS, NPTS), -(NY // 8), NY // 8 + 1)
    offset_z = jax.random.randint(subkeys[5], (NATOMS, NPTS), -(NZ // 8), NZ // 8 + 1)
    coord_x = jnp.clip(centre_x + offset_x, 0, NX - 1)
    coord_y = (centre_y + offset_y) % NY
    coord_z = (centre_z + offset_z) % NZ
    flat_points = (coord_x * (NY * NZ) + coord_y * NZ + coord_z).astype(jnp.int32)
    return (flat_points, offset_x, offset_y, offset_z, subkeys[6])


def draw_proj_index(key, part):
    flat_points, offset_x, offset_y, offset_z, factor_key = support_geometry(key)
    return flat_points


def draw_proj_value(key, part):
    flat_points, offset_x, offset_y, offset_z, factor_key = support_geometry(key)
    reach_x = float(PL)
    reach_z = float(max(NZ // 8, 1))
    scaled_x = offset_x.astype(jnp.float32) / reach_x
    scaled_y = offset_y.astype(jnp.float32)
    scaled_z = offset_z.astype(jnp.float32) / reach_z
    distance = scaled_x * scaled_x + scaled_y * scaled_y + scaled_z * scaled_z
    profile = jnp.exp(-distance)
    factor = jax.random.uniform(factor_key, (NATOMS, NPTS), jnp.float32, 0.5, 1.5)
    unscaled = profile * factor
    return (unscaled / jnp.sqrt(jnp.sum(unscaled * unscaled, axis=1, keepdims=True))).astype(jnp.float32)


def levels(own_key, shape, shards, smallest, top_value):
    level, own = 1.0, jax.random.fold_in(own_key, 6)
    for axis_at, parts in shards:
        heights = jnp.exp(jax.random.uniform(jax.random.fold_in(own, axis_at), (parts,), jnp.float32, smallest / len(shards), top_value / len(shards)))
        level = level * jnp.repeat(heights, shape[axis_at] // parts).reshape([-1 if axis == axis_at else 1 for axis in range(len(shape))])
    return level


def noise(rng, dims, width, bound, shards=(), dtype=jnp.bfloat16):
    drawn = width * jax.random.normal(rng, dims, jnp.float32)
    if shards:
        drawn = drawn * levels(rng, dims, shards, -0.22, 0.18)
    return jnp.clip(drawn, -bound, bound).astype(dtype)


def setup_inputs(seed: int = 0) -> dict:
    seeds = jax.random.split(jax.random.key(seed), 6)
    states = noise(seeds[0], (NSTATES, NX, NY, NZ), 1.0, 6.0, ((0, 4), (1, 64)), jnp.float32)
    potential = jnp.clip(jax.random.uniform(seeds[1], (NX, NY, NZ), jnp.float32, -1.0, 1.0) * levels(seeds[1], (NX, NY, NZ), ((0, 64),), -0.4, 0.0), -1.0, 1.0)
    proj_index = draw_proj_index(jax.random.fold_in(seeds[5], 71), 0)
    proj_value = draw_proj_value(jax.random.fold_in(seeds[5], 71), 0)
    proj_strength = jnp.clip(jnp.exp(jax.random.uniform(seeds[4], (NATOMS,), jnp.float32, math.log(0.5), math.log(4.0))), 0.5, 4.0)
    return {"states": states, "potential": potential, "proj_index": proj_index, "proj_value": proj_value, "proj_strength": proj_strength}


stencil_weights = (-205.0 / 72.0, 1.6, -0.2, 8.0 / 315.0, -1.0 / 560.0)
filter_centre = 10.0
filter_half = 6.0


def kinetic(padded):
    extent = padded.shape[-3] - 2 * RADIUS
    middle = padded[..., RADIUS:RADIUS + extent, :, :]
    grid_rows = middle.shape[-2]
    grid_cols = middle.shape[-1]
    pad_widths = [(0, 0)] * (middle.ndim - 2) + [(RADIUS, RADIUS), (RADIUS, RADIUS)]
    padded_yz = jnp.pad(middle, pad_widths)
    summed = 3.0 * stencil_weights[0] * middle
    for shift_by in range(1, RADIUS + 1):
        neighbours = padded[..., RADIUS + shift_by:RADIUS + shift_by + extent, :, :] + padded[..., RADIUS - shift_by:RADIUS - shift_by + extent, :, :]
        neighbours = neighbours + padded_yz[..., RADIUS + shift_by:RADIUS + shift_by + grid_rows, RADIUS:RADIUS + grid_cols] + padded_yz[..., RADIUS - shift_by:RADIUS - shift_by + grid_rows, RADIUS:RADIUS + grid_cols]
        neighbours = neighbours + padded_yz[..., RADIUS:RADIUS + grid_rows, RADIUS + shift_by:RADIUS + shift_by + grid_cols] + padded_yz[..., RADIUS:RADIUS + grid_rows, RADIUS - shift_by:RADIUS - shift_by + grid_cols]
        summed = summed + stencil_weights[shift_by] * neighbours
    return -0.5 * summed


def reference(states, potential, proj_index, proj_value, proj_strength):
    flat_index = proj_index.astype(jnp.int32)

    def apply_h(field):
        padded = jnp.pad(field, ((RADIUS, RADIUS), (0, 0), (0, 0)))
        kinetic_v = kinetic(padded)
        flat_v = field.reshape(-1)
        picked = flat_v[flat_index]
        coeffs = jnp.sum(proj_value * picked, axis=1)
        added = (proj_strength * coeffs)[:, None] * proj_value
        nonlocal_v = jnp.zeros_like(flat_v).at[flat_index.reshape(-1)].add(added.reshape(-1))
        return kinetic_v + potential * field + nonlocal_v.reshape(field.shape)

    def filter_one(state):
        previous = state
        current = (apply_h(state) - filter_centre * state) / filter_half
        for degree_k in range(1, DEGREE):
            following = 2.0 * (apply_h(current) - filter_centre * current) / filter_half - previous
            previous = current
            current = following
        return current, apply_h(current)

    filtered, images = lax.map(filter_one, states)
    flat_y = filtered.reshape(NSTATES, NPOINTS)
    flat_h = images.reshape(NSTATES, NPOINTS)
    gram = jnp.dot(flat_y, flat_y.T, precision=lax.Precision.HIGHEST) / float(NPOINTS)
    hamiltonian = jnp.dot(flat_h, flat_y.T, precision=lax.Precision.HIGHEST) / float(NPOINTS)
    return filtered, gram, hamiltonian
```

```python
import functools

import jax
import jax.numpy as jnp
from jax import lax
from jax.experimental import pallas as pl
from jax.experimental.pallas import tpu as pltpu
from jax.sharding import PartitionSpec as P

RADIUS = 4
DEGREE = 4
WINDOW = 17

stencil_weights = (-205.0 / 72.0, 1.6, -0.2, 8.0 / 315.0, -1.0 / 560.0)
filter_centre = 10.0
filter_half = 6.0

VMEM = pl.BlockSpec(memory_space=pltpu.VMEM)
SMEM = pl.BlockSpec(memory_space=pltpu.SMEM)
NT = (((1,), (1,)), ((), ()))


def call(kernel, name, out_shape, in_specs, out_specs, scratch=(), flops=4_000_000, nbytes=4_000_000):
    return pl.pallas_call(
        kernel,
        name=name,
        out_shape=out_shape,
        in_specs=in_specs,
        out_specs=out_specs,
        scratch_shapes=list(scratch),
        compiler_params=pltpu.CompilerParams(vmem_limit_bytes=20 << 20),
        cost_estimate=pl.CostEstimate(flops=flops, bytes_accessed=nbytes, transcendentals=0),
    )


def build_kernel(planes, info, idx, val, blocks, table):
    base = info[0] * planes
    atoms, points = idx.shape
    cells = 8 * 128
    table[2, 0] = 0
    table[2, 1] = info[0]

    def pick(a, carry):
        low = info[8 + a]
        high = info[8 + atoms + a]

        @pl.when((high >= base) & (low < base + planes))
        def _():
            n = table[2, 0]
            table[0, n] = a
            table[1, n] = jnp.clip(low - base, 0, planes - WINDOW)
            table[2, 0] = n + 1

        return carry

    lax.fori_loop(0, atoms, pick, 0)

    def build(n, carry):
        a = table[0, n]
        rel = idx[pl.ds(a, 1), :] - (base + table[1, n]) * cells
        inside = (rel >= 0) & (rel < WINDOW * cells)
        w = jnp.where(inside, val[pl.ds(a, 1), :], 0.0)
        row = rel >> 7
        col = rel & 127
        hit = lax.broadcasted_iota(jnp.int32, (WINDOW * 8, points), 0) == row
        cols = (lax.broadcasted_iota(jnp.int32, (128, points), 0) == col).astype(jnp.float32).astype(jnp.bfloat16)
        w1 = w.astype(jnp.bfloat16).astype(jnp.float32)
        w2 = (w - w1).astype(jnp.bfloat16).astype(jnp.float32)
        w3 = w - w1 - w2
        total = None
        for part in (w3, w2, w1):
            rows = jnp.where(hit, part, 0.0).astype(jnp.bfloat16)
            term = lax.dot_general(rows, cols, NT, preferred_element_type=jnp.float32)
            total = term if total is None else total + term
        blocks[pl.ds(n, 1)] = total.reshape(1, WINDOW, 8, 128)
        return carry

    lax.fori_loop(0, table[2, 0], build, 0)


def coefficients(table, field, blocks, sums):
    sums[...] = jnp.zeros_like(sums)

    def one(n, carry):
        a = table[0, n]
        st = table[1, n]
        acc = [None, None]
        for i in range(WINDOW):
            b = blocks[n, i]
            for s in range(2):
                t = b * field(s, st + i)
                acc[s] = t if acc[s] is None else acc[s] + t
        for s in range(2):
            sums[s, pl.ds(a, 1), :] = jnp.sum(acc[s], axis=0, keepdims=True)
        return carry

    lax.fori_loop(0, table[2, 0], one, 0)
    ones = jnp.ones((8, 128), jnp.float32)
    return [
        lax.dot_general(ones, sums[s], NT, precision=lax.Precision.HIGHEST, preferred_element_type=jnp.float32)
        for s in range(2)
    ]


def first_kernel(table, y, blocks, up, down, sums):
    slabs = y.shape[0]
    parts = coefficients(table, lambda s, p: y[p >> 3, s, p & 7], blocks, sums)
    for s in range(2):
        up[s, 0:4] = y[slabs - 1, s, 4:8]
        down[s, 0:4] = y[0, s, 0:4]
        up[s, 4] = parts[s]
        down[s, 4] = parts[s]


def lane_weights():
    lane = lax.broadcasted_iota(jnp.int32, (8, 128), 1)
    out = []
    for k in range(1, RADIUS + 1):
        c = stencil_weights[k]
        out.append((k, jnp.where(lane >= k, c, 0.0)))
        out.append((128 - k, jnp.where(lane < 128 - k, c, 0.0)))
    return out


def row_weights():
    row = lax.broadcasted_iota(jnp.int32, (8, 128), 0)
    out = []
    for r in range(1, 8):
        near = stencil_weights[r] if r <= RADIUS else 0.0
        far = stencil_weights[8 - r] if 8 - r <= RADIUS else 0.0
        out.append((r, jnp.where(row >= r, near, far)))
    return out


def step_kernel(mode, table, y, *refs):
    has_prev = mode in ("middle", "last")
    refs = list(refs)
    prev = refs.pop(0) if has_prev else None
    v, blocks, strength, below, above, own = refs[:6]
    refs = refs[6:]
    if mode == "image":
        (send, pad, new, splat) = refs
        alpha, sigma = 1.0, 0.0
    else:
        (out, up, down, pad, new, splat, sums) = refs
        alpha = (1.0 if mode == "first" else 2.0) / filter_half
        sigma = filter_centre
    slabs = y.shape[0]
    planes = slabs * 8
    z = table[2, 1]
    has_low = z > 0
    has_high = z < lax.axis_size("grid") // slabs - 1
    for s in range(2):
        pad[s, 0:4] = jnp.where(has_low, below[s, 0:4], 0.0)
        pad[s, planes + 4 : planes + 8] = jnp.where(has_high, above[s, 0:4], 0.0)
        for j in range(slabs):
            pad[s, 4 + 8 * j : 12 + 8 * j] = y[j, s]
    half = -0.5 * alpha
    lanes = [(k, w * half) for k, w in lane_weights()]
    rows = [(k, w * half) for k, w in row_weights()]
    centre = half * 3.0 * stencil_weights[0] - alpha * sigma

    def block(j, carry):
        for s in range(2):
            line = [pad[s, 8 * j + t] for t in range(16)]
            for t in range(8):
                mid = line[t + 4]
                acc = (alpha * v[j, 2, t] + centre) * mid
                for k in range(1, RADIUS + 1):
                    acc = acc + (half * stencil_weights[k]) * (line[t + 4 + k] + line[t + 4 - k])
                for k, w in rows:
                    acc = acc + w * pltpu.roll(mid, k, 0)
                for k, w in lanes:
                    acc = acc + w * pltpu.roll(mid, k, 1)
                if has_prev:
                    acc = acc - prev[j, s, t]
                new[s, 8 * j + t] = acc
        return carry

    lax.fori_loop(0, slabs, block, 0)

    for s in range(2):
        total = (own[s, 4] + below[s, 4] + above[s, 4]) * strength[...] * alpha
        splat[s] = jnp.transpose(jnp.broadcast_to(total[0:1], (128, 128)))

    def spread(n, carry):
        a = table[0, n]
        st = table[1, n]
        c = [jnp.broadcast_to(splat[s, pl.ds(a, 1), :], (8, 128)) for s in range(2)]
        for i in range(WINDOW):
            b = blocks[n, i]
            for s in range(2):
                new[s, st + i] = new[s, st + i] + c[s] * b
        return carry

    lax.fori_loop(0, table[2, 0], spread, 0)

    if mode == "image":
        for s in range(2):
            for j in range(slabs):
                for t in range(8):
                    d = (t // 2) * slabs + j
                    q = 8 * (t % 2)
                    send[d, s, 0, q : q + 8] = y[j, s, t]
                    send[d, s, 1, q : q + 8] = new[s, 8 * j + t]
    else:
        parts = coefficients(table, lambda s, p: new[s, p], blocks, sums)
        for s in range(2):
            for j in range(slabs):
                out[j, s] = new[s, 8 * j : 8 * j + 8]
            up[s, 0:4] = new[s, planes - 4 : planes]
            down[s, 0:4] = new[s, 0:4]
            up[s, 4] = parts[s]
            down[s, 4] = parts[s]


def product_kernel(states, got, out):
    total = None
    for r in range(16):
        f = got[pl.ds(r, states, stride=32), :]
        h = got[pl.ds(16 + r, states, stride=32), :]
        term = lax.dot_general(
            jnp.concatenate([f, h], axis=0), f, NT, precision=lax.Precision.HIGHEST, preferred_element_type=jnp.float32
        )
        total = term if total is None else total + term
    out[...] = jnp.concatenate([total[0:states], total[states : 2 * states]], axis=1)


def per_device(states, potential, proj_index, proj_value, proj_strength):
    f32 = jnp.float32
    count, depth, ny, nz = states.shape
    atoms = proj_index.shape[0]
    grid = lax.axis_size("grid")
    bands = lax.axis_size("band")
    group = 8
    zs = grid // group
    per = count // group
    planes = group * depth
    in_plane = [[z * group + j for j in range(group)] for z in range(zs)]
    along_z = [[z * group + j for z in range(zs)] for j in range(group)]
    whole_plane = [[b * grid + z * group + j for b in range(bands) for j in range(group)] for z in range(zs)]

    z = lax.axis_index("grid") // group
    support = proj_index >> 10
    info = jnp.concatenate(
        [jnp.full((8,), z, jnp.int32), jnp.min(support, axis=1), jnp.max(support, axis=1)]
    ).astype(jnp.int32)
    blocks, table = call(
        functools.partial(build_kernel, planes),
        "build",
        (jax.ShapeDtypeStruct((atoms, WINDOW, ny, nz), f32), jax.ShapeDtypeStruct((3, 128), jnp.int32)),
        [SMEM, VMEM, VMEM],
        (VMEM, SMEM),
    )(info, proj_index, proj_value)

    parcel = jnp.concatenate(
        [
            states.reshape(group, per, depth, ny, nz),
            jnp.broadcast_to(potential, (group, 1, depth, ny, nz)),
        ],
        axis=1,
    )
    start = lax.all_to_all(parcel, "grid", 0, 0, axis_index_groups=in_plane, tiled=True)

    field = jax.ShapeDtypeStruct((group, per, depth, ny, nz), f32)
    message = jax.ShapeDtypeStruct((per, 5, ny, nz), f32)
    sums = pltpu.VMEM((per, atoms, 128), f32)
    pad = pltpu.VMEM((per, planes + 8, ny, nz), f32)
    new = pltpu.VMEM((per, planes, ny, nz), f32)
    strength = proj_strength.reshape(1, atoms)

    up, down = call(first_kernel, "first", (message, message), [SMEM, VMEM, VMEM], (VMEM, VMEM), [sums])(
        table, start, blocks
    )

    def exchange(up, down):
        below = lax.ppermute(up, "grid", [(i, (i + group) % grid) for i in range(grid)])
        above = lax.ppermute(down, "grid", [(i, (i - group) % grid) for i in range(grid)])
        return below, above

    previous, current = None, start
    for k in range(DEGREE):
        mode = "first" if k == 0 else ("last" if k == DEGREE - 1 else "middle")
        below, above = exchange(up, down)
        args = [table, current] + ([previous] if k else []) + [start, blocks, strength, below, above, up]
        following, up, down = call(
            functools.partial(step_kernel, mode),
            "step",
            (field, message, message),
            [SMEM] + [VMEM] * (len(args) - 1),
            (VMEM,) * 3,
            [pad, new, sums, sums],
        )(*args)
        previous, current = current, following

    below, above = exchange(up, down)
    filtered = lax.all_to_all(current, "grid", 0, 0, axis_index_groups=in_plane, tiled=True).reshape(states.shape)
    send = call(
        functools.partial(step_kernel, "image"),
        "image",
        jax.ShapeDtypeStruct((bands * group, per, 2, 2 * ny, nz), f32),
        [SMEM] + [VMEM] * 7,
        VMEM,
        [pad, new, sums],
    )(table, current, start, blocks, strength, below, above, up)
    got = lax.all_to_all(send, ("band", "grid"), 0, 0, axis_index_groups=whole_plane, tiled=True)
    everyone = bands * count
    part = call(
        functools.partial(product_kernel, everyone),
        "product",
        jax.ShapeDtypeStruct((everyone, 2 * everyone), f32),
        [VMEM],
        VMEM,
    )(got.reshape(everyone * 32, nz))

    rows = lax.all_to_all(part.reshape(bands, count, 2 * everyone), "band", 0, 0, tiled=True).sum(axis=0)
    for members in (in_plane, along_z):
        copies = jnp.broadcast_to(rows, (group, *rows.shape))
        rows = lax.all_to_all(copies, "grid", 0, 0, axis_index_groups=members, tiled=True).sum(axis=0)
    rows = rows / float(grid * depth * ny * nz)
    return filtered, rows[:, :everyone], rows[:, everyone:]


def solution(mesh):
    in_specs = (P("band", "grid", None, None), P("grid", None, None), P(), P(), P())
    out_specs = (P("band", "grid", None, None), P("band", None), P("band", None))
    return jax.shard_map(
        per_device, mesh=mesh, in_specs=in_specs, out_specs=out_specs, check_vma=False
    )
```

```python
import functools

import jax
import jax.numpy as jnp
from jax import lax
from jax.experimental import pallas as pl
from jax.experimental.pallas import tpu as pltpu
from jax.sharding import PartitionSpec as P

RADIUS = 4
DEGREE = 4
WINDOW = 17

stencil_weights = (-205.0 / 72.0, 1.6, -0.2, 8.0 / 315.0, -1.0 / 560.0)
filter_centre = 10.0
filter_half = 6.0

VMEM = pl.BlockSpec(memory_space=pltpu.VMEM)
SMEM = pl.BlockSpec(memory_space=pltpu.SMEM)
HBM = pl.BlockSpec(memory_space=pltpu.HBM)
NT = (((1,), (1,)), ((), ()))


def call(kernel, name, out_shape, in_specs, out_specs, scratch=(), flops=4_000_000, nbytes=2_000_000, vmem=6):
    return pl.pallas_call(
        kernel,
        name=name,
        out_shape=out_shape,
        in_specs=in_specs,
        out_specs=out_specs,
        scratch_shapes=list(scratch),
        compiler_params=pltpu.CompilerParams(vmem_limit_bytes=vmem << 20),
        cost_estimate=pl.CostEstimate(flops=flops, bytes_accessed=nbytes, transcendentals=0),
    )


def far(x):
    return pltpu.with_memory_space_constraint(x, pltpu.HBM)


def parcel_kernel(states, potential, out, held, extra, sems):
    group = out.shape[0]
    local = pltpu.make_async_copy(potential, extra, sems.at[2, 0])
    loads = [pltpu.make_async_copy(states.at[j], held.at[j], sems.at[0, j]) for j in range(group)]
    stores = [pltpu.make_async_copy(held.at[j], out.at[j, 0:2], sems.at[1, j]) for j in range(group)]
    extras = [pltpu.make_async_copy(extra, out.at[j, 2], sems.at[3, j]) for j in range(group)]
    for c in [local] + loads:
        c.start()
    local.wait()
    for c in extras:
        c.start()
    for j in range(group):
        loads[j].wait()
        stores[j].start()
    for c in extras + stores:
        c.wait()


def build_kernel(planes, info, idx_far, val_far, blocks_far, table, idx, val, blocks, sems):
    loads = [pltpu.make_async_copy(idx_far, idx, sems.at[0]), pltpu.make_async_copy(val_far, val, sems.at[1])]
    for c in loads:
        c.start()
    base = info[1, 1] * planes
    atoms, points = idx.shape
    cells = 8 * 128

    def pick(a, n):
        entry = info[0, a]
        table[0, n] = entry
        return n + (entry >= 0).astype(jnp.int32)

    count = lax.fori_loop(0, atoms, pick, jnp.int32(0), unroll=16)
    table[0, count] = atoms * 256
    pairs = (count + 1) >> 1
    table[1, 0] = pairs
    table[1, 1] = info[1, 1]
    table[1, 2] = info[1, 2]
    for c in loads:
        c.wait()
    sub = lax.broadcasted_iota(jnp.int32, (WINDOW * 8, points), 0)
    lane = lax.broadcasted_iota(jnp.int32, (128, points), 0)

    def pair(m, carry):
        for n in (2 * m, 2 * m + 1):
            entry = table[0, n]
            a = jnp.minimum(entry >> 8, atoms - 1)
            rel = idx[pl.ds(a, 1), :] - (base + (entry & 255)) * cells
            inside = (rel >= 0) & (rel < WINDOW * cells) & (n < count)
            w = jnp.where(inside, val[pl.ds(a, 1), :], 0.0)
            hit = sub == (rel >> 7)
            cols = (lane == (rel & 127)).astype(jnp.float32).astype(jnp.bfloat16)
            w1 = w.astype(jnp.bfloat16).astype(jnp.float32)
            w2 = (w - w1).astype(jnp.bfloat16).astype(jnp.float32)
            w3 = w - w1 - w2
            total = None
            for part in (w3, w2, w1):
                rows = jnp.where(hit, part, 0.0).astype(jnp.bfloat16)
                term = lax.dot_general(rows, cols, NT, preferred_element_type=jnp.float32)
                total = term if total is None else total + term
            blocks[pl.ds(n, 1)] = total.reshape(1, WINDOW, 8, 128)
        store(m).start()
        return carry

    def store(m):
        two = pl.ds(2 * m, 2)
        return pltpu.make_async_copy(blocks.at[two], blocks_far.at[two], sems.at[2 + m])

    def stored(m, carry):
        store(m).wait()
        return carry

    lax.fori_loop(0, pairs, pair, 0)
    lax.fori_loop(0, pairs, stored, 0)


def coefficients(table, field, blocks, sums, ready=None):
    atoms = blocks.shape[0]
    sums[...] = jnp.zeros_like(sums)

    def pair(m, carry):
        if ready is not None:
            ready(m)
        for n in (2 * m, 2 * m + 1):
            entry = table[0, n]
            b = blocks[n]
            for s in range(2):
                v = field[s, pl.ds(entry & 255, WINDOW)]
                sums[s, pl.ds(entry >> 8, 1), :] = jnp.sum(jnp.sum(b * v, axis=0), axis=0, keepdims=True)
        return carry

    lax.fori_loop(0, table[1, 0], pair, 0)
    ones = jnp.ones((8, 128), jnp.float32)
    return [
        lax.dot_general(
            ones, sums[s, 0:atoms], NT, precision=lax.Precision.HIGHEST, preferred_element_type=jnp.float32
        )
        for s in range(2)
    ]


def fill_messages(y, parts, up, down):
    planes = y.shape[1]
    for s in range(2):
        up[s, 0:4] = y[s, planes - 4 : planes]
        down[s, 0:4] = y[s, 0:4]
        up[s, 4] = parts[s]
        down[s, 4] = parts[s]


def first_kernel(table, got, blocks_far, y, up, down, blocks, sums, sems):
    def load(m):
        two = pl.ds(2 * m, 2)
        return pltpu.make_async_copy(blocks_far.at[two], blocks.at[two], sems.at[m])

    def begin(m, carry):
        load(m).start()
        return carry

    lax.fori_loop(0, table[1, 0], begin, 0)
    for s in range(2):
        for j in range(got.shape[0]):
            y[s, 8 * j : 8 * j + 8] = got[j, s]
    fill_messages(y, coefficients(table, y, blocks, sums, lambda m: load(m).wait()), up, down)


def lane_weights():
    lane = lax.broadcasted_iota(jnp.int32, (8, 128), 1)
    out = []
    for k in range(1, RADIUS + 1):
        c = stencil_weights[k]
        out.append((k, jnp.where(lane >= k, c, 0.0)))
        out.append((128 - k, jnp.where(lane < 128 - k, c, 0.0)))
    return out


def row_weights():
    row = lax.broadcasted_iota(jnp.int32, (8, 128), 0)
    out = []
    for r in range(1, 8):
        near = stencil_weights[r] if r <= RADIUS else 0.0
        far = stencil_weights[8 - r] if 8 - r <= RADIUS else 0.0
        out.append((r, jnp.where(row >= r, near, far)))
    return out


def scales(mode):
    if mode == "image":
        return 1.0, 0.0
    return (1.0 if mode == "first" else 2.0) / filter_half, filter_centre


def stencil_kernel(mode, y, *refs):
    has_prev = mode == "later"
    prev, v, out, pad = refs if has_prev else (None, *refs)
    alpha, sigma = scales(mode)
    planes = y.shape[1]
    for s in range(2):
        pad[s, 0:4] = jnp.zeros((4, 8, 128), jnp.float32)
        pad[s, 4 : planes + 4] = y[s]
        pad[s, planes + 4 : planes + 8] = jnp.zeros((4, 8, 128), jnp.float32)
    half = -0.5 * alpha
    lanes = [(k, w * half) for k, w in lane_weights()]
    rows = [(k, w * half) for k, w in row_weights()]
    centre = half * 3.0 * stencil_weights[0] - alpha * sigma

    def block(j, carry):
        for s in range(2):
            line = [pad[s, 8 * j + t] for t in range(16)]
            for t in range(8):
                mid = line[t + 4]
                acc = (alpha * v[j, 2, t] + centre) * mid
                for k in range(1, RADIUS + 1):
                    acc = acc + (half * stencil_weights[k]) * (line[t + 4 + k] + line[t + 4 - k])
                for k, w in rows:
                    acc = acc + w * pltpu.roll(mid, k, 0)
                for k, w in lanes:
                    acc = acc + w * pltpu.roll(mid, k, 1)
                if has_prev:
                    acc = acc - prev[s, 8 * j + t]
                out[s, 8 * j + t] = acc
        return carry

    lax.fori_loop(0, planes // 8, block, 0)


def finish_kernel(mode, table, partial, blocks, strength, below, above, own, *refs):
    alpha, sigma = scales(mode)
    if mode == "image":
        y, send, new, splat = refs
    else:
        new, up, down, splat, sums = refs
    planes = partial.shape[1]
    atoms = blocks.shape[0]
    z = table[1, 1]
    has_low = z > 0
    has_high = z < lax.axis_size("grid") // (planes // 8) - 1
    half = -0.5 * alpha

    for s in range(2):
        total = (own[s, 4] + below[s, 4] + above[s, 4]) * strength[...] * alpha
        splat[s, 0:atoms] = jnp.transpose(jnp.broadcast_to(total[0:1], (128, 128)))
        splat[s, atoms : atoms + 8] = jnp.zeros((8, 128), jnp.float32)

    new[...] = partial[...]
    for s in range(2):
        low = [jnp.where(has_low, below[s, i], 0.0) for i in range(4)]
        high = [jnp.where(has_high, above[s, i], 0.0) for i in range(4)]
        for t in range(4):
            for side, edge in ((low, 0), (high, 1)):
                acc = None
                for k in range(t + 1, RADIUS + 1):
                    value = side[t - k + 4] if edge == 0 else side[k - t - 1]
                    term = (half * stencil_weights[k]) * value
                    acc = term if acc is None else acc + term
                p = t if edge == 0 else planes - 1 - t
                new[s, p] = new[s, p] + acc

    def spread(m, carry):
        for n in (2 * m, 2 * m + 1):
            entry = table[0, n]
            b = blocks[n]
            window = pl.ds(entry & 255, WINDOW)
            for s in range(2):
                c = jnp.broadcast_to(splat[s, pl.ds(entry >> 8, 1), :], (8, 128))
                new[s, window] = new[s, window] + c * b
        return carry

    lax.fori_loop(0, table[1, 0], spread, 0)

    if mode == "image":
        for s in range(2):
            for p in range(planes):
                j, t = divmod(p, 8)
                d = (t // 2) * (planes // 8) + j
                q = 8 * (t % 2)
                send[d, s, 0, q : q + 8] = y[s, p]
                send[d, s, 1, q : q + 8] = new[s, p]
    else:
        fill_messages(new, coefficients(table, new, blocks, sums), up, down)


def product_kernel(table, got, keep, give, rows):
    states = rows.shape[0]
    total = None
    for r in range(0, 16, 2):
        f = [got[pl.ds(r + i, states, stride=32), :] for i in range(2)]
        h = [got[pl.ds(16 + r + i, states, stride=32), :] for i in range(2)]
        f = jnp.concatenate(f, axis=1)
        left = jnp.concatenate([f, jnp.concatenate(h, axis=1)], axis=0)
        term = lax.dot_general(
            left, f, NT, precision=lax.Precision.HIGHEST, preferred_element_type=jnp.float32
        )
        total = term if total is None else total + term
    rows[...] = jnp.concatenate([total[0:states], total[states : 2 * states]], axis=1)
    band = table[1, 2]
    size = keep.shape[1]
    for other in range(2):
        chip = band ^ (2 * other)
        keep[other] = rows[pl.ds(pl.multiple_of(chip * size, size), size), :]
        give[other] = rows[pl.ds(pl.multiple_of((chip ^ 1) * size, size), size), :]


def pack_kernel(y, parts, out):
    rows = parts[0]
    for k in range(1, parts.shape[0]):
        rows = rows + parts[k]
    for j in range(out.shape[0]):
        out[j, 0:8] = y[0, 8 * j : 8 * j + 8]
        out[j, 8:16] = y[1, 8 * j : 8 * j + 8]
        out[j, 16] = rows[0:8]
        out[j, 17] = rows[8:16]


def unpack_kernel(scale, got, filtered, gram, hamiltonian):
    width = gram.shape[1]
    for half in range(2):
        rows = got[0, 16 + half]
        for j in range(1, got.shape[0]):
            rows = rows + got[j, 16 + half]
        rows = rows * scale
        gram[8 * half : 8 * half + 8] = rows[:, 0:width]
        hamiltonian[8 * half : 8 * half + 8] = rows[:, width : 2 * width]
    for j in range(got.shape[0]):
        filtered[2 * j] = got[j, 0:8]
        filtered[2 * j + 1] = got[j, 8:16]


def per_device(states, potential, proj_index, proj_value, proj_strength):
    f32 = jnp.float32
    shape = jax.ShapeDtypeStruct
    count, depth, ny, nz = states.shape
    atoms = proj_index.shape[0]
    grid = lax.axis_size("grid")
    bands = lax.axis_size("band")
    group = 8
    zs = grid // group
    per = count // group
    planes = group * depth
    everyone = bands * count
    in_plane = [[z * group + j for j in range(group)] for z in range(zs)]
    along_z = [[z * group + j for z in range(zs)] for j in range(group)]
    whole_plane = [[b * grid + z * group + j for b in range(bands) for j in range(group)] for z in range(zs)]

    parcel = call(
        parcel_kernel,
        "parcel",
        pltpu.HBM((group, 3, depth, ny, nz), f32),
        [HBM] * 2,
        HBM,
        [
            pltpu.VMEM((group, per, depth, ny, nz), f32),
            pltpu.VMEM((depth, ny, nz), f32),
            pltpu.SemaphoreType.DMA((4, group)),
        ],
    )(far(states.reshape(group, per, depth, ny, nz)), far(potential))
    start = lax.all_to_all(parcel, "grid", 0, 0, axis_index_groups=in_plane, tiled=True)

    place = lax.axis_index("grid") // group
    support = proj_index >> 10
    low = jnp.min(support, axis=1) - place * planes
    high = jnp.max(support, axis=1) - place * planes
    entry = jnp.arange(atoms, dtype=jnp.int32) * 256 + jnp.clip(low, 0, planes - WINDOW)
    entry = jnp.where((high >= 0) & (low < planes), entry, -1)
    lane = jnp.arange(atoms, dtype=jnp.int32)
    where = jnp.where(lane == 1, place, jnp.where(lane == 2, lax.axis_index("band"), 0))
    info = jnp.stack([entry, where]).astype(jnp.int32)

    field = shape((per, planes, ny, nz), f32)
    message = shape((per, 5, ny, nz), f32)
    sums = pltpu.VMEM((per, atoms + 8, 128), f32)
    pad = pltpu.VMEM((per, planes + 8, ny, nz), f32)
    new = pltpu.VMEM(field.shape, f32)
    strength = proj_strength.reshape(1, atoms)

    block = (atoms, WINDOW, ny, nz)
    blocks_far, table = call(
        functools.partial(build_kernel, planes),
        "build",
        (pltpu.HBM(block, f32), shape((2, 256), jnp.int32)),
        [SMEM, HBM, HBM],
        (HBM, SMEM),
        [
            pltpu.VMEM(proj_index.shape, jnp.int32),
            pltpu.VMEM(proj_value.shape, f32),
            pltpu.VMEM(block, f32),
            pltpu.SemaphoreType.DMA((2 + atoms // 2,)),
        ],
        vmem=16,
    )(info, far(proj_index), far(proj_value))
    current, up, down, blocks = call(
        first_kernel,
        "first",
        (field, message, message, shape(block, f32)),
        [SMEM, VMEM, HBM],
        (VMEM,) * 4,
        [sums, pltpu.SemaphoreType.DMA((atoms // 2,))],
        vmem=16,
    )(table, start, far(blocks_far))

    def exchange(up, down):
        below = lax.ppermute(up, "grid", [(i, (i + group) % grid) for i in range(grid)])
        above = lax.ppermute(down, "grid", [(i, (i - group) % grid) for i in range(grid)])
        return below, above

    def local(mode, *arrays):
        return call(
            functools.partial(stencil_kernel, mode), "stencil", field, [VMEM] * len(arrays), VMEM, [pad]
        )(*arrays)

    previous = None
    for k in range(DEGREE):
        mode = "later" if k else "first"
        below, above = exchange(up, down)
        partial = local(mode, current, *([previous] if k else []), start)
        following, up, down = call(
            functools.partial(finish_kernel, mode),
            "finish",
            (field, message, message),
            [SMEM] + [VMEM] * 6,
            (VMEM,) * 3,
            [sums, sums],
        )(table, partial, blocks, strength, below, above, up)
        previous, current = current, following

    below, above = exchange(up, down)
    send = call(
        functools.partial(finish_kernel, "image"),
        "image",
        shape((bands * group, per, 2, 2 * ny, nz), f32),
        [SMEM] + [VMEM] * 7,
        VMEM,
        [new, sums],
    )(table, local("image", current, start), blocks, strength, below, above, up, current)
    got = lax.all_to_all(send, ("band", "grid"), 0, 0, axis_index_groups=whole_plane, tiled=True)
    half = shape((2, count, 2 * everyone), f32)
    keep, give = call(
        product_kernel, "product", (half, half), [SMEM, VMEM], (VMEM, VMEM), [pltpu.VMEM((everyone, 2 * everyone), f32)]
    )(table, got.reshape(everyone * 32, nz))
    keep = keep + lax.ppermute(give, "band", [(i, i ^ 1) for i in range(bands)])
    rows = keep[0] + lax.ppermute(keep[1], "band", [(i, i ^ 2) for i in range(bands)])

    copies = jnp.broadcast_to(rows, (zs, *rows.shape))
    copies = lax.all_to_all(copies, "grid", 0, 0, axis_index_groups=along_z, tiled=True)
    packed = call(pack_kernel, "pack", shape((group, 18, ny, nz), f32), [VMEM, VMEM], VMEM)(current, copies)
    packed = lax.all_to_all(packed, "grid", 0, 0, axis_index_groups=in_plane, tiled=True)
    square = shape((count, everyone), f32)
    return call(
        functools.partial(unpack_kernel, 1.0 / float(grid * depth * ny * nz)),
        "unpack",
        (shape(states.shape, f32), square, square),
        [VMEM],
        (VMEM,) * 3,
    )(packed)


def solution(mesh):
    in_specs = (P("band", "grid", None, None), P("grid", None, None), P(), P(), P())
    out_specs = (P("band", "grid", None, None), P("band", None), P("band", None))
    return jax.shard_map(
        per_device, mesh=mesh, in_specs=in_specs, out_specs=out_specs, check_vma=False
    )
```

```python
import functools

import jax
import jax.numpy as jnp
from jax import lax
from jax.experimental import pallas as pl
from jax.experimental.pallas import tpu as pltpu
from jax.sharding import PartitionSpec as P

RADIUS = 4
DEGREE = 4
WINDOW = 17
BATCH = 4

stencil_weights = (-205.0 / 72.0, 1.6, -0.2, 8.0 / 315.0, -1.0 / 560.0)
filter_centre = 10.0
filter_half = 6.0

VMEM = pl.BlockSpec(memory_space=pltpu.VMEM)
SMEM = pl.BlockSpec(memory_space=pltpu.SMEM)
HBM = pl.BlockSpec(memory_space=pltpu.HBM)
NT = (((1,), (1,)), ((), ()))


def call(kernel, name, out_shape, in_specs, out_specs, scratch=(), flops=4_000_000, nbytes=2_000_000, vmem=6):
    return pl.pallas_call(
        kernel,
        name=name,
        out_shape=out_shape,
        in_specs=in_specs,
        out_specs=out_specs,
        scratch_shapes=list(scratch),
        compiler_params=pltpu.CompilerParams(vmem_limit_bytes=vmem << 20),
        cost_estimate=pl.CostEstimate(flops=flops, bytes_accessed=nbytes, transcendentals=0),
    )


def far(x):
    return pltpu.with_memory_space_constraint(x, pltpu.HBM)


def parcel_kernel(states, potential, out, held, extra, sems):
    group = out.shape[0]
    local = pltpu.make_async_copy(potential, extra, sems.at[2, 0])
    loads = [pltpu.make_async_copy(states.at[j], held.at[j], sems.at[0, j]) for j in range(group)]
    stores = [pltpu.make_async_copy(held.at[j], out.at[j, 0:2], sems.at[1, j]) for j in range(group)]
    extras = [pltpu.make_async_copy(extra, out.at[j, 2], sems.at[3, j]) for j in range(group)]
    for c in [local] + loads:
        c.start()
    local.wait()
    for c in extras:
        c.start()
    for j in range(group):
        loads[j].wait()
        stores[j].start()
    for c in extras + stores:
        c.wait()


def build_kernel(planes, info, idx_far, val_far, blocks_far, table, idx, val, blocks, sems):
    loads = [pltpu.make_async_copy(idx_far, idx, sems.at[0]), pltpu.make_async_copy(val_far, val, sems.at[1])]
    for c in loads:
        c.start()
    base = info[1, 1] * planes
    atoms, points = idx.shape
    cells = 8 * 128

    def pick(a, n):
        entry = info[0, a]
        table[0, n] = entry
        return n + (entry >= 0).astype(jnp.int32)

    count = lax.fori_loop(0, atoms, pick, jnp.int32(0), unroll=16)
    for i in range(BATCH - 1):
        table[0, count + i] = atoms * 256
    batches = (count + BATCH - 1) // BATCH
    table[1, 0] = batches
    table[1, 1] = info[1, 1]
    for c in loads:
        c.wait()
    sub = lax.broadcasted_iota(jnp.int32, (WINDOW * 8, points), 0)
    lane = lax.broadcasted_iota(jnp.int32, (128, points), 0)

    def batch(m, carry):
        for n in [BATCH * m + i for i in range(BATCH)]:
            entry = table[0, n]
            a = jnp.minimum(entry >> 8, atoms - 1)
            rel = idx[pl.ds(a, 1), :] - (base + (entry & 255)) * cells
            inside = (rel >= 0) & (rel < WINDOW * cells) & (n < count)
            w = jnp.where(inside, val[pl.ds(a, 1), :], 0.0)
            hit = sub == (rel >> 7)
            cols = (lane == (rel & 127)).astype(jnp.float32).astype(jnp.bfloat16)
            w1 = w.astype(jnp.bfloat16).astype(jnp.float32)
            w2 = (w - w1).astype(jnp.bfloat16).astype(jnp.float32)
            w3 = w - w1 - w2
            total = None
            for part in (w3, w2, w1):
                rows = jnp.where(hit, part, 0.0).astype(jnp.bfloat16)
                term = lax.dot_general(rows, cols, NT, preferred_element_type=jnp.float32)
                total = term if total is None else total + term
            blocks[pl.ds(n, 1)] = total.reshape(1, WINDOW, 8, 128)
        store(m).start()
        return carry

    def store(m):
        some = pl.ds(BATCH * m, BATCH)
        return pltpu.make_async_copy(blocks.at[some], blocks_far.at[some], sems.at[2 + m])

    def stored(m, carry):
        store(m).wait()
        return carry

    lax.fori_loop(0, batches, batch, 0)
    lax.fori_loop(0, batches, stored, 0)


def coefficients(table, field, blocks, sums, ready=None):
    atoms = blocks.shape[0]
    sums[...] = jnp.zeros_like(sums)

    def batch(m, carry):
        if ready is not None:
            ready(m)
        for n in [BATCH * m + i for i in range(BATCH)]:
            entry = table[0, n]
            b = blocks[n]
            for s in range(2):
                v = field[s, pl.ds(entry & 255, WINDOW)]
                sums[s, pl.ds(entry >> 8, 1), :] = jnp.sum(jnp.sum(b * v, axis=0), axis=0, keepdims=True)
        return carry

    lax.fori_loop(0, table[1, 0], batch, 0)
    ones = jnp.ones((8, 128), jnp.float32)
    return [
        lax.dot_general(
            ones, sums[s, 0:atoms], NT, precision=lax.Precision.HIGHEST, preferred_element_type=jnp.float32
        )
        for s in range(2)
    ]


def fill_messages(y, parts, up, down):
    planes = y.shape[1]
    for s in range(2):
        up[s, 0:4] = y[s, planes - 4 : planes]
        down[s, 0:4] = y[s, 0:4]
        up[s, 4] = parts[s]
        down[s, 4] = parts[s]


def first_kernel(table, got, blocks_far, y, up, down, blocks, sums, sems):
    def load(m):
        some = pl.ds(BATCH * m, BATCH)
        return pltpu.make_async_copy(blocks_far.at[some], blocks.at[some], sems.at[m])

    def begin(m, carry):
        load(m).start()
        return carry

    lax.fori_loop(0, table[1, 0], begin, 0)
    for s in range(2):
        for j in range(got.shape[0]):
            y[s, 8 * j : 8 * j + 8] = got[j, s]
    fill_messages(y, coefficients(table, y, blocks, sums, lambda m: load(m).wait()), up, down)


def lane_weights():
    lane = lax.broadcasted_iota(jnp.int32, (8, 128), 1)
    out = []
    for k in range(1, RADIUS + 1):
        c = stencil_weights[k]
        out.append((k, jnp.where(lane >= k, c, 0.0)))
        out.append((128 - k, jnp.where(lane < 128 - k, c, 0.0)))
    return out


def row_weights():
    row = lax.broadcasted_iota(jnp.int32, (8, 128), 0)
    out = []
    for r in range(1, 8):
        near = stencil_weights[r] if r <= RADIUS else 0.0
        far = stencil_weights[8 - r] if 8 - r <= RADIUS else 0.0
        out.append((r, jnp.where(row >= r, near, far)))
    return out


def scales(mode):
    if mode == "image":
        return 1.0, 0.0
    return (1.0 if mode == "first" else 2.0) / filter_half, filter_centre


def stencil_kernel(mode, y, *refs):
    has_prev = mode == "later"
    prev, v, out, pad = refs if has_prev else (None, *refs)
    alpha, sigma = scales(mode)
    planes = y.shape[1]
    for s in range(2):
        pad[s, 0:4] = jnp.zeros((4, 8, 128), jnp.float32)
        pad[s, 4 : planes + 4] = y[s]
        pad[s, planes + 4 : planes + 8] = jnp.zeros((4, 8, 128), jnp.float32)
    half = -0.5 * alpha
    lanes = [(k, w * half) for k, w in lane_weights()]
    rows = [(k, w * half) for k, w in row_weights()]
    centre = half * 3.0 * stencil_weights[0] - alpha * sigma

    def block(j, carry):
        for s in range(2):
            line = [pad[s, 8 * j + t] for t in range(16)]
            for t in range(8):
                mid = line[t + 4]
                acc = (alpha * v[j, 2, t] + centre) * mid
                for k in range(1, RADIUS + 1):
                    acc = acc + (half * stencil_weights[k]) * (line[t + 4 + k] + line[t + 4 - k])
                for k, w in rows:
                    acc = acc + w * pltpu.roll(mid, k, 0)
                for k, w in lanes:
                    acc = acc + w * pltpu.roll(mid, k, 1)
                if has_prev:
                    acc = acc - prev[s, 8 * j + t]
                out[s, 8 * j + t] = acc
        return carry

    lax.fori_loop(0, planes // 8, block, 0)


def finish_kernel(mode, table, partial, blocks, strength, below, above, own, *refs):
    alpha, sigma = scales(mode)
    if mode == "image":
        y, send, new, splat = refs
    else:
        new, up, down, splat, sums = refs
    planes = partial.shape[1]
    atoms = blocks.shape[0]
    z = table[1, 1]
    has_low = z > 0
    has_high = z < lax.axis_size("grid") // (planes // 8) - 1
    half = -0.5 * alpha

    for s in range(2):
        total = (own[s, 4] + below[s, 4] + above[s, 4]) * strength[...] * alpha
        splat[s, 0:atoms] = jnp.transpose(jnp.broadcast_to(total[0:1], (128, 128)))
        splat[s, atoms : atoms + 8] = jnp.zeros((8, 128), jnp.float32)

    new[...] = partial[...]
    for s in range(2):
        low = [jnp.where(has_low, below[s, i], 0.0) for i in range(4)]
        high = [jnp.where(has_high, above[s, i], 0.0) for i in range(4)]
        for t in range(4):
            for side, edge in ((low, 0), (high, 1)):
                acc = None
                for k in range(t + 1, RADIUS + 1):
                    value = side[t - k + 4] if edge == 0 else side[k - t - 1]
                    term = (half * stencil_weights[k]) * value
                    acc = term if acc is None else acc + term
                p = t if edge == 0 else planes - 1 - t
                new[s, p] = new[s, p] + acc

    def spread(m, carry):
        for n in [BATCH * m + i for i in range(BATCH)]:
            entry = table[0, n]
            b = blocks[n]
            window = pl.ds(entry & 255, WINDOW)
            for s in range(2):
                c = jnp.broadcast_to(splat[s, pl.ds(entry >> 8, 1), :], (8, 128))
                new[s, window] = new[s, window] + c * b
        return carry

    lax.fori_loop(0, table[1, 0], spread, 0)

    if mode == "image":
        for s in range(2):
            for p in range(planes):
                j, t = divmod(p, 8)
                d = (t // 2) * (planes // 8) + j
                q = 8 * (t % 2)
                send[d, s, 0, q : q + 8] = y[s, p]
                send[d, s, 1, q : q + 8] = new[s, p]
    else:
        fill_messages(new, coefficients(table, new, blocks, sums), up, down)


def product_kernel(got, rows):
    states = rows.shape[0]
    total = None
    for r in range(0, 16, 2):
        f = [got[pl.ds(r + i, states, stride=32), :] for i in range(2)]
        h = [got[pl.ds(16 + r + i, states, stride=32), :] for i in range(2)]
        f = jnp.concatenate(f, axis=1)
        left = jnp.concatenate([f, jnp.concatenate(h, axis=1)], axis=0)
        term = lax.dot_general(
            left, f, NT, precision=lax.Precision.HIGHEST, preferred_element_type=jnp.float32
        )
        total = term if total is None else total + term
    rows[...] = jnp.concatenate([total[0:states], total[states : 2 * states]], axis=1)


def pack_kernel(y, parts, out):
    rows = parts[0]
    for k in range(1, parts.shape[0]):
        rows = rows + parts[k]
    for j in range(out.shape[0]):
        out[j, 0:8] = y[0, 8 * j : 8 * j + 8]
        out[j, 8:16] = y[1, 8 * j : 8 * j + 8]
        out[j, 16] = rows[0:8]
        out[j, 17] = rows[8:16]


def unpack_kernel(scale, got, filtered, gram, hamiltonian):
    width = gram.shape[1]
    for half in range(2):
        rows = got[0, 16 + half]
        for j in range(1, got.shape[0]):
            rows = rows + got[j, 16 + half]
        rows = rows * scale
        gram[8 * half : 8 * half + 8] = rows[:, 0:width]
        hamiltonian[8 * half : 8 * half + 8] = rows[:, width : 2 * width]
    for j in range(got.shape[0]):
        filtered[2 * j] = got[j, 0:8]
        filtered[2 * j + 1] = got[j, 8:16]


def per_device(states, potential, proj_index, proj_value, proj_strength):
    f32 = jnp.float32
    shape = jax.ShapeDtypeStruct
    count, depth, ny, nz = states.shape
    atoms = proj_index.shape[0]
    grid = lax.axis_size("grid")
    bands = lax.axis_size("band")
    group = 8
    zs = grid // group
    per = count // group
    planes = group * depth
    everyone = bands * count
    in_plane = [[z * group + j for j in range(group)] for z in range(zs)]
    along_z = [[z * group + j for z in range(zs)] for j in range(group)]
    whole_plane = [[b * grid + z * group + j for b in range(bands) for j in range(group)] for z in range(zs)]

    parcel = call(
        parcel_kernel,
        "parcel",
        pltpu.HBM((group, 3, depth, ny, nz), f32),
        [HBM] * 2,
        HBM,
        [
            pltpu.VMEM((group, per, depth, ny, nz), f32),
            pltpu.VMEM((depth, ny, nz), f32),
            pltpu.SemaphoreType.DMA((4, group)),
        ],
    )(far(states.reshape(group, per, depth, ny, nz)), far(potential))
    start = lax.all_to_all(parcel, "grid", 0, 0, axis_index_groups=in_plane, tiled=True)

    place = lax.axis_index("grid") // group
    support = proj_index >> 10
    low = jnp.min(support, axis=1) - place * planes
    high = jnp.max(support, axis=1) - place * planes
    entry = jnp.arange(atoms, dtype=jnp.int32) * 256 + jnp.clip(low, 0, planes - WINDOW)
    entry = jnp.where((high >= 0) & (low < planes), entry, -1)
    info = jnp.stack([entry, jnp.full((atoms,), place)]).astype(jnp.int32)

    field = shape((per, planes, ny, nz), f32)
    message = shape((per, 5, ny, nz), f32)
    sums = pltpu.VMEM((per, atoms + 8, 128), f32)
    pad = pltpu.VMEM((per, planes + 8, ny, nz), f32)
    new = pltpu.VMEM(field.shape, f32)
    strength = proj_strength.reshape(1, atoms)

    block = (atoms, WINDOW, ny, nz)
    blocks_far, table = call(
        functools.partial(build_kernel, planes),
        "build",
        (pltpu.HBM(block, f32), shape((2, 256), jnp.int32)),
        [SMEM, HBM, HBM],
        (HBM, SMEM),
        [
            pltpu.VMEM(proj_index.shape, jnp.int32),
            pltpu.VMEM(proj_value.shape, f32),
            pltpu.VMEM(block, f32),
            pltpu.SemaphoreType.DMA((2 + atoms // BATCH,)),
        ],
        vmem=16,
    )(info, far(proj_index), far(proj_value))
    current, up, down, blocks = call(
        first_kernel,
        "first",
        (field, message, message, shape(block, f32)),
        [SMEM, VMEM, HBM],
        (VMEM,) * 4,
        [sums, pltpu.SemaphoreType.DMA((atoms // BATCH,))],
        vmem=16,
    )(table, start, far(blocks_far))

    def exchange(up, down):
        below = lax.ppermute(up, "grid", [(i, (i + group) % grid) for i in range(grid)])
        above = lax.ppermute(down, "grid", [(i, (i - group) % grid) for i in range(grid)])
        return below, above

    def local(mode, *arrays):
        return call(
            functools.partial(stencil_kernel, mode), "stencil", field, [VMEM] * len(arrays), VMEM, [pad]
        )(*arrays)

    previous = None
    for k in range(DEGREE):
        mode = "later" if k else "first"
        below, above = exchange(up, down)
        partial = local(mode, current, *([previous] if k else []), start)
        following, up, down = call(
            functools.partial(finish_kernel, mode),
            "finish",
            (field, message, message),
            [SMEM] + [VMEM] * 6,
            (VMEM,) * 3,
            [sums, sums],
        )(table, partial, blocks, strength, below, above, up)
        previous, current = current, following

    below, above = exchange(up, down)
    send = call(
        functools.partial(finish_kernel, "image"),
        "image",
        shape((bands * group, per, 2, 2 * ny, nz), f32),
        [SMEM] + [VMEM] * 7,
        VMEM,
        [new, sums],
    )(table, local("image", current, start), blocks, strength, below, above, up, current)
    got = lax.all_to_all(send, ("band", "grid"), 0, 0, axis_index_groups=whole_plane, tiled=True)
    part = call(product_kernel, "product", shape((everyone, 2 * everyone), f32), [VMEM], VMEM)(
        got.reshape(everyone * 32, nz)
    )
    band = lax.axis_index("band")
    part = part + lax.ppermute(part, "band", [(i, i ^ 1) for i in range(bands)])
    mine = lax.dynamic_slice_in_dim(part, band * count, count, axis=0)
    other = lax.dynamic_slice_in_dim(part, (band ^ 2) * count, count, axis=0)
    rows = mine + lax.ppermute(other, "band", [(i, i ^ 2) for i in range(bands)])

    copies = jnp.broadcast_to(rows, (zs, *rows.shape))
    copies = lax.all_to_all(copies, "grid", 0, 0, axis_index_groups=along_z, tiled=True)
    packed = call(pack_kernel, "pack", shape((group, 18, ny, nz), f32), [VMEM, VMEM], VMEM)(current, copies)
    packed = lax.all_to_all(packed, "grid", 0, 0, axis_index_groups=in_plane, tiled=True)
    square = shape((count, everyone), f32)
    return call(
        functools.partial(unpack_kernel, 1.0 / float(grid * depth * ny * nz)),
        "unpack",
        (shape(states.shape, f32), square, square),
        [VMEM],
        (VMEM,) * 3,
    )(packed)


def solution(mesh):
    in_specs = (P("band", "grid", None, None), P("grid", None, None), P(), P(), P())
    out_specs = (P("band", "grid", None, None), P("band", None), P("band", None))
    return jax.shard_map(
        per_device, mesh=mesh, in_specs=in_specs, out_specs=out_specs, check_vma=False
    )
```

```python
import functools

import jax
import jax.numpy as jnp
from jax import lax
from jax.experimental import pallas as pl
from jax.experimental.pallas import tpu as pltpu
from jax.sharding import PartitionSpec as P

RADIUS = 4
DEGREE = 4
WINDOW = 17
BATCH = 4

stencil_weights = (-205.0 / 72.0, 1.6, -0.2, 8.0 / 315.0, -1.0 / 560.0)
filter_centre = 10.0
filter_half = 6.0

VMEM = pl.BlockSpec(memory_space=pltpu.VMEM)
SMEM = pl.BlockSpec(memory_space=pltpu.SMEM)
HBM = pl.BlockSpec(memory_space=pltpu.HBM)
NT = (((1,), (1,)), ((), ()))


def call(kernel, name, out_shape, in_specs, out_specs, scratch=(), flops=4_000_000, nbytes=2_000_000, vmem=6):
    return pl.pallas_call(
        kernel,
        name=name,
        out_shape=out_shape,
        in_specs=in_specs,
        out_specs=out_specs,
        scratch_shapes=list(scratch),
        compiler_params=pltpu.CompilerParams(vmem_limit_bytes=vmem << 20),
        cost_estimate=pl.CostEstimate(flops=flops, bytes_accessed=nbytes, transcendentals=0),
    )


def far(x):
    return pltpu.with_memory_space_constraint(x, pltpu.HBM)


def parcel_kernel(states, potential, out, held, extra, sems):
    group = out.shape[0]
    local = pltpu.make_async_copy(potential, extra, sems.at[2, 0])
    loads = [pltpu.make_async_copy(states.at[j], held.at[j], sems.at[0, j]) for j in range(group)]
    stores = [pltpu.make_async_copy(held.at[j], out.at[j, 0:2], sems.at[1, j]) for j in range(group)]
    extras = [pltpu.make_async_copy(extra, out.at[j, 2], sems.at[3, j]) for j in range(group)]
    for c in [local] + loads:
        c.start()
    local.wait()
    for c in extras:
        c.start()
    for j in range(group):
        loads[j].wait()
        stores[j].start()
    for c in extras + stores:
        c.wait()


def build_kernel(planes, info, idx_far, val_far, blocks_far, table, idx, val, blocks, sems):
    loads = [pltpu.make_async_copy(idx_far, idx, sems.at[0]), pltpu.make_async_copy(val_far, val, sems.at[1])]
    for c in loads:
        c.start()
    base = info[1, 1] * planes
    atoms, points = idx.shape
    cells = 8 * 128

    def pick(a, n):
        entry = info[0, a]
        table[0, n] = entry
        return n + (entry >= 0).astype(jnp.int32)

    count = lax.fori_loop(0, atoms, pick, jnp.int32(0), unroll=16)
    for i in range(BATCH - 1):
        table[0, count + i] = atoms * 256
    batches = (count + BATCH - 1) // BATCH
    table[1, 0] = batches
    table[1, 1] = info[1, 1]
    for c in loads:
        c.wait()
    sub = lax.broadcasted_iota(jnp.int32, (WINDOW * 8, points), 0)
    lane = lax.broadcasted_iota(jnp.int32, (128, points), 0)

    def batch(m, carry):
        for n in [BATCH * m + i for i in range(BATCH)]:
            entry = table[0, n]
            a = jnp.minimum(entry >> 8, atoms - 1)
            rel = idx[pl.ds(a, 1), :] - (base + (entry & 255)) * cells
            inside = (rel >= 0) & (rel < WINDOW * cells) & (n < count)
            w = jnp.where(inside, val[pl.ds(a, 1), :], 0.0)
            hit = sub == (rel >> 7)
            cols = (lane == (rel & 127)).astype(jnp.float32).astype(jnp.bfloat16)
            w1 = w.astype(jnp.bfloat16).astype(jnp.float32)
            w2 = (w - w1).astype(jnp.bfloat16).astype(jnp.float32)
            w3 = w - w1 - w2
            total = None
            for part in (w3, w2, w1):
                rows = jnp.where(hit, part, 0.0).astype(jnp.bfloat16)
                term = lax.dot_general(rows, cols, NT, preferred_element_type=jnp.float32)
                total = term if total is None else total + term
            blocks[pl.ds(n, 1)] = total.reshape(1, WINDOW, 8, 128)
        store(m).start()
        return carry

    def store(m):
        some = pl.ds(BATCH * m, BATCH)
        return pltpu.make_async_copy(blocks.at[some], blocks_far.at[some], sems.at[2 + m])

    def stored(m, carry):
        store(m).wait()
        return carry

    lax.fori_loop(0, batches, batch, 0)
    lax.fori_loop(0, batches, stored, 0)


def coefficients(table, field, blocks, sums, ready=None):
    atoms = blocks.shape[0]
    sums[...] = jnp.zeros_like(sums)

    def batch(m, carry):
        if ready is not None:
            ready(m)
        for n in [BATCH * m + i for i in range(BATCH)]:
            entry = table[0, n]
            b = blocks[n]
            for s in range(2):
                v = field[s, pl.ds(entry & 255, WINDOW)]
                sums[s, pl.ds(entry >> 8, 1), :] = jnp.sum(jnp.sum(b * v, axis=0), axis=0, keepdims=True)
        return carry

    lax.fori_loop(0, table[1, 0], batch, 0)
    ones = jnp.ones((8, 128), jnp.float32)
    return [
        lax.dot_general(
            ones, sums[s, 0:atoms], NT, precision=lax.Precision.HIGHEST, preferred_element_type=jnp.float32
        )
        for s in range(2)
    ]


def fill_messages(y, parts, up, down):
    planes = y.shape[1]
    for s in range(2):
        up[s, 0:4] = y[s, planes - 4 : planes]
        down[s, 0:4] = y[s, 0:4]
        up[s, 4] = parts[s]
        down[s, 4] = parts[s]


def first_kernel(table, got, blocks_far, y, up, down, blocks, sums, sems):
    def load(m):
        some = pl.ds(BATCH * m, BATCH)
        return pltpu.make_async_copy(blocks_far.at[some], blocks.at[some], sems.at[m])

    def begin(m, carry):
        load(m).start()
        return carry

    lax.fori_loop(0, table[1, 0], begin, 0)
    for s in range(2):
        for j in range(got.shape[0]):
            y[s, 8 * j : 8 * j + 8] = got[j, s]
    fill_messages(y, coefficients(table, y, blocks, sums, lambda m: load(m).wait()), up, down)


def lane_weights():
    lane = lax.broadcasted_iota(jnp.int32, (8, 128), 1)
    out = []
    for k in range(1, RADIUS + 1):
        c = stencil_weights[k]
        out.append((k, jnp.where(lane >= k, c, 0.0)))
        out.append((128 - k, jnp.where(lane < 128 - k, c, 0.0)))
    return out


def row_weights():
    row = lax.broadcasted_iota(jnp.int32, (8, 128), 0)
    out = []
    for r in range(1, 8):
        near = stencil_weights[r] if r <= RADIUS else 0.0
        far = stencil_weights[8 - r] if 8 - r <= RADIUS else 0.0
        out.append((r, jnp.where(row >= r, near, far)))
    return out


def scales(mode):
    if mode == "image":
        return 1.0, 0.0
    return (1.0 if mode == "first" else 2.0) / filter_half, filter_centre


def stencil_kernel(mode, y, *refs):
    has_prev = mode == "later"
    prev, v, out, pad = refs if has_prev else (None, *refs)
    alpha, sigma = scales(mode)
    planes = y.shape[1]
    for s in range(2):
        pad[s, 0:4] = jnp.zeros((4, 8, 128), jnp.float32)
        pad[s, 4 : planes + 4] = y[s]
        pad[s, planes + 4 : planes + 8] = jnp.zeros((4, 8, 128), jnp.float32)
    half = -0.5 * alpha
    lanes = [(k, w * half) for k, w in lane_weights()]
    rows = [(k, w * half) for k, w in row_weights()]
    centre = half * 3.0 * stencil_weights[0] - alpha * sigma

    def block(j, carry):
        for s in range(2):
            line = [pad[s, 8 * j + t] for t in range(16)]
            for t in range(8):
                mid = line[t + 4]
                acc = (alpha * v[j, 2, t] + centre) * mid
                for k in range(1, RADIUS + 1):
                    acc = acc + (half * stencil_weights[k]) * (line[t + 4 + k] + line[t + 4 - k])
                for k, w in rows:
                    acc = acc + w * pltpu.roll(mid, k, 0)
                for k, w in lanes:
                    acc = acc + w * pltpu.roll(mid, k, 1)
                if has_prev:
                    acc = acc - prev[s, 8 * j + t]
                out[s, 8 * j + t] = acc
        return carry

    lax.fori_loop(0, planes // 8, block, 0)


def finish_kernel(mode, table, partial, blocks, strength, below, above, own, *refs):
    alpha, sigma = scales(mode)
    if mode == "image":
        y, send, new, splat = refs
    else:
        new, up, down, splat, sums = refs
    planes = partial.shape[1]
    atoms = blocks.shape[0]
    z = table[1, 1]
    has_low = z > 0
    has_high = z < lax.axis_size("grid") // (planes // 8) - 1
    half = -0.5 * alpha

    for s in range(2):
        total = (own[s, 4] + below[s, 4] + above[s, 4]) * strength[...] * alpha
        splat[s, 0:atoms] = jnp.transpose(jnp.broadcast_to(total[0:1], (128, 128)))
        splat[s, atoms : atoms + 8] = jnp.zeros((8, 128), jnp.float32)

    new[...] = partial[...]
    for s in range(2):
        low = [jnp.where(has_low, below[s, i], 0.0) for i in range(4)]
        high = [jnp.where(has_high, above[s, i], 0.0) for i in range(4)]
        for t in range(4):
            for side, edge in ((low, 0), (high, 1)):
                acc = None
                for k in range(t + 1, RADIUS + 1):
                    value = side[t - k + 4] if edge == 0 else side[k - t - 1]
                    term = (half * stencil_weights[k]) * value
                    acc = term if acc is None else acc + term
                p = t if edge == 0 else planes - 1 - t
                new[s, p] = new[s, p] + acc

    def spread(m, carry):
        for n in [BATCH * m + i for i in range(BATCH)]:
            entry = table[0, n]
            b = blocks[n]
            window = pl.ds(entry & 255, WINDOW)
            for s in range(2):
                c = jnp.broadcast_to(splat[s, pl.ds(entry >> 8, 1), :], (8, 128))
                new[s, window] = new[s, window] + c * b
        return carry

    lax.fori_loop(0, table[1, 0], spread, 0)

    if mode == "image":
        for s in range(2):
            for p in range(planes):
                j, t = divmod(p, 8)
                d = (t // 2) * (planes // 8) + j
                q = 8 * (t % 2)
                send[d, s, 0, q : q + 8] = y[s, p]
                send[d, s, 1, q : q + 8] = new[s, p]
    else:
        fill_messages(new, coefficients(table, new, blocks, sums), up, down)


def product_kernel(got, rows):
    states = rows.shape[0]
    total = None
    for r in range(0, 16, 2):
        f = [got[pl.ds(r + i, states, stride=32), :] for i in range(2)]
        h = [got[pl.ds(16 + r + i, states, stride=32), :] for i in range(2)]
        f = jnp.concatenate(f, axis=1)
        left = jnp.concatenate([f, jnp.concatenate(h, axis=1)], axis=0)
        term = lax.dot_general(
            left, f, NT, precision=lax.Precision.HIGHEST, preferred_element_type=jnp.float32
        )
        total = term if total is None else total + term
    rows[...] = jnp.concatenate([total[0:states], total[states : 2 * states]], axis=1)


def pack_kernel(y, parts, out):
    rows = parts[0]
    for k in range(1, parts.shape[0]):
        rows = rows + parts[k]
    for j in range(out.shape[0]):
        out[j, 0:8] = y[0, 8 * j : 8 * j + 8]
        out[j, 8:16] = y[1, 8 * j : 8 * j + 8]
        out[j, 16] = rows[0:8]
        out[j, 17] = rows[8:16]


def unpack_kernel(scale, got, filtered, gram, hamiltonian):
    width = gram.shape[1]
    for half in range(2):
        rows = got[0, 16 + half]
        for j in range(1, got.shape[0]):
            rows = rows + got[j, 16 + half]
        rows = rows * scale
        gram[8 * half : 8 * half + 8] = rows[:, 0:width]
        hamiltonian[8 * half : 8 * half + 8] = rows[:, width : 2 * width]
    for j in range(got.shape[0]):
        filtered[2 * j] = got[j, 0:8]
        filtered[2 * j + 1] = got[j, 8:16]


def per_device(states, potential, proj_index, proj_value, proj_strength):
    f32 = jnp.float32
    shape = jax.ShapeDtypeStruct
    count, depth, ny, nz = states.shape
    atoms = proj_index.shape[0]
    grid = lax.axis_size("grid")
    bands = lax.axis_size("band")
    group = 8
    zs = grid // group
    per = count // group
    planes = group * depth
    everyone = bands * count
    in_plane = [[z * group + j for j in range(group)] for z in range(zs)]
    along_z = [[z * group + j for z in range(zs)] for j in range(group)]
    whole_plane = [[b * grid + z * group + j for b in range(bands) for j in range(group)] for z in range(zs)]

    parcel = call(
        parcel_kernel,
        "parcel",
        pltpu.HBM((group, 3, depth, ny, nz), f32),
        [HBM] * 2,
        HBM,
        [
            pltpu.VMEM((group, per, depth, ny, nz), f32),
            pltpu.VMEM((depth, ny, nz), f32),
            pltpu.SemaphoreType.DMA((4, group)),
        ],
    )(far(states.reshape(group, per, depth, ny, nz)), far(potential))
    start = lax.all_to_all(parcel, "grid", 0, 0, axis_index_groups=in_plane, tiled=True)

    place = lax.axis_index("grid") // group
    support = proj_index >> 10
    low = jnp.min(support, axis=1) - place * planes
    high = jnp.max(support, axis=1) - place * planes
    entry = jnp.arange(atoms, dtype=jnp.int32) * 256 + jnp.clip(low, 0, planes - WINDOW)
    entry = jnp.where((high >= 0) & (low < planes), entry, -1)
    info = jnp.stack([entry, jnp.full((atoms,), place)]).astype(jnp.int32)

    field = shape((per, planes, ny, nz), f32)
    message = shape((per, 5, ny, nz), f32)
    sums = pltpu.VMEM((per, atoms + 8, 128), f32)
    pad = pltpu.VMEM((per, planes + 8, ny, nz), f32)
    new = pltpu.VMEM(field.shape, f32)
    strength = proj_strength.reshape(1, atoms)

    block = (atoms, WINDOW, ny, nz)
    blocks_far, table = call(
        functools.partial(build_kernel, planes),
        "build",
        (pltpu.HBM(block, f32), pltpu.SMEM((2, 256), jnp.int32)),
        [SMEM, HBM, HBM],
        (HBM, SMEM),
        [
            pltpu.VMEM(proj_index.shape, jnp.int32),
            pltpu.VMEM(proj_value.shape, f32),
            pltpu.VMEM(block, f32),
            pltpu.SemaphoreType.DMA((2 + atoms // BATCH,)),
        ],
        vmem=16,
    )(info, far(proj_index), far(proj_value))
    table = pltpu.with_memory_space_constraint(table, pltpu.SMEM)
    current, up, down, blocks = call(
        first_kernel,
        "first",
        (field, message, message, shape(block, f32)),
        [SMEM, VMEM, HBM],
        (VMEM,) * 4,
        [sums, pltpu.SemaphoreType.DMA((atoms // BATCH,))],
        vmem=16,
    )(table, start, far(blocks_far))

    def exchange(up, down):
        below = lax.ppermute(up, "grid", [(i, (i + group) % grid) for i in range(grid)])
        above = lax.ppermute(down, "grid", [(i, (i - group) % grid) for i in range(grid)])
        return below, above

    def local(mode, *arrays):
        return call(
            functools.partial(stencil_kernel, mode), "stencil", field, [VMEM] * len(arrays), VMEM, [pad]
        )(*arrays)

    previous = None
    for k in range(DEGREE):
        mode = "later" if k else "first"
        below, above = exchange(up, down)
        partial = local(mode, current, *([previous] if k else []), start)
        following, up, down = call(
            functools.partial(finish_kernel, mode),
            "finish",
            (field, message, message),
            [SMEM] + [VMEM] * 6,
            (VMEM,) * 3,
            [sums, sums],
        )(table, partial, blocks, strength, below, above, up)
        previous, current = current, following

    below, above = exchange(up, down)
    send = call(
        functools.partial(finish_kernel, "image"),
        "image",
        shape((bands * group, per, 2, 2 * ny, nz), f32),
        [SMEM] + [VMEM] * 7,
        VMEM,
        [new, sums],
    )(table, local("image", current, start), blocks, strength, below, above, up, current)
    got = lax.all_to_all(send, ("band", "grid"), 0, 0, axis_index_groups=whole_plane, tiled=True)
    part = call(product_kernel, "product", shape((everyone, 2 * everyone), f32), [VMEM], VMEM)(
        got.reshape(everyone * 32, nz)
    )
    band = lax.axis_index("band")
    part = part + lax.ppermute(part, "band", [(i, i ^ 1) for i in range(bands)])
    mine = lax.dynamic_slice_in_dim(part, band * count, count, axis=0)
    other = lax.dynamic_slice_in_dim(part, (band ^ 2) * count, count, axis=0)
    rows = mine + lax.ppermute(other, "band", [(i, i ^ 2) for i in range(bands)])

    copies = jnp.broadcast_to(rows, (zs, *rows.shape))
    copies = lax.all_to_all(copies, "grid", 0, 0, axis_index_groups=along_z, tiled=True)
    packed = call(pack_kernel, "pack", shape((group, 18, ny, nz), f32), [VMEM, VMEM], VMEM)(current, copies)
    packed = lax.all_to_all(packed, "grid", 0, 0, axis_index_groups=in_plane, tiled=True)
    square = shape((count, everyone), f32)
    return call(
        functools.partial(unpack_kernel, 1.0 / float(grid * depth * ny * nz)),
        "unpack",
        (shape(states.shape, f32), square, square),
        [VMEM],
        (VMEM,) * 3,
    )(packed)


def solution(mesh):
    in_specs = (P("band", "grid", None, None), P("grid", None, None), P(), P(), P())
    out_specs = (P("band", "grid", None, None), P("band", None), P("band", None))
    return jax.shard_map(
        per_device, mesh=mesh, in_specs=in_specs, out_specs=out_specs, check_vma=False
    )
```

```python
import functools

import jax
import jax.numpy as jnp
from jax import lax
from jax.experimental import pallas as pl
from jax.experimental.pallas import tpu as pltpu
from jax.sharding import PartitionSpec as P

RADIUS = 4
DEGREE = 4
WINDOW = 17
BATCH = 4

stencil_weights = (-205.0 / 72.0, 1.6, -0.2, 8.0 / 315.0, -1.0 / 560.0)
filter_centre = 10.0
filter_half = 6.0

VMEM = pl.BlockSpec(memory_space=pltpu.VMEM)
SMEM = pl.BlockSpec(memory_space=pltpu.SMEM)
HBM = pl.BlockSpec(memory_space=pltpu.HBM)
NT = (((1,), (1,)), ((), ()))


def call(kernel, name, out_shape, in_specs, out_specs, scratch=(), flops=4_000_000, nbytes=2_000_000, vmem=6):
    return pl.pallas_call(
        kernel,
        name=name,
        out_shape=out_shape,
        in_specs=in_specs,
        out_specs=out_specs,
        scratch_shapes=list(scratch),
        compiler_params=pltpu.CompilerParams(vmem_limit_bytes=vmem << 20),
        cost_estimate=pl.CostEstimate(flops=flops, bytes_accessed=nbytes, transcendentals=0),
    )


def far(x):
    return pltpu.with_memory_space_constraint(x, pltpu.HBM)


def parcel_kernel(states, potential, out, held, extra, sems):
    group = out.shape[0]
    local = pltpu.make_async_copy(potential, extra, sems.at[2, 0])
    loads = [pltpu.make_async_copy(states.at[j], held.at[j], sems.at[0, j]) for j in range(group)]
    stores = [pltpu.make_async_copy(held.at[j], out.at[j, 0:2], sems.at[1, j]) for j in range(group)]
    extras = [pltpu.make_async_copy(extra, out.at[j, 2], sems.at[3, j]) for j in range(group)]
    for c in [local] + loads:
        c.start()
    local.wait()
    for c in extras:
        c.start()
    for j in range(group):
        loads[j].wait()
        stores[j].start()
    for c in extras + stores:
        c.wait()


def build_kernel(planes, info, idx_far, val_far, blocks_far, table, idx, val, blocks, sems):
    loads = [pltpu.make_async_copy(idx_far, idx, sems.at[0]), pltpu.make_async_copy(val_far, val, sems.at[1])]
    for c in loads:
        c.start()
    base = info[1, 1] * planes
    atoms, points = idx.shape
    cells = 8 * 128

    def pick(a, n):
        entry = info[0, a]
        table[0, n] = entry
        return n + (entry >= 0).astype(jnp.int32)

    count = lax.fori_loop(0, atoms, pick, jnp.int32(0), unroll=16)
    for i in range(BATCH - 1):
        table[0, count + i] = atoms * 256
    batches = (count + BATCH - 1) // BATCH
    table[1, 0] = batches
    table[1, 1] = info[1, 1]
    for c in loads:
        c.wait()
    sub = lax.broadcasted_iota(jnp.int32, (WINDOW * 8, points), 0)
    lane = lax.broadcasted_iota(jnp.int32, (128, points), 0)

    def batch(m, carry):
        for n in [BATCH * m + i for i in range(BATCH)]:
            entry = table[0, n]
            a = jnp.minimum(entry >> 8, atoms - 1)
            rel = idx[pl.ds(a, 1), :] - (base + (entry & 255)) * cells
            inside = (rel >= 0) & (rel < WINDOW * cells) & (n < count)
            w = jnp.where(inside, val[pl.ds(a, 1), :], 0.0)
            hit = sub == (rel >> 7)
            cols = (lane == (rel & 127)).astype(jnp.float32).astype(jnp.bfloat16)
            w1 = w.astype(jnp.bfloat16).astype(jnp.float32)
            w2 = (w - w1).astype(jnp.bfloat16).astype(jnp.float32)
            w3 = w - w1 - w2
            total = None
            for part in (w3, w2, w1):
                rows = jnp.where(hit, part, 0.0).astype(jnp.bfloat16)
                term = lax.dot_general(rows, cols, NT, preferred_element_type=jnp.float32)
                total = term if total is None else total + term
            blocks[pl.ds(n, 1)] = total.reshape(1, WINDOW, 8, 128)
        store(m).start()
        return carry

    def store(m):
        some = pl.ds(BATCH * m, BATCH)
        return pltpu.make_async_copy(blocks.at[some], blocks_far.at[some], sems.at[2 + m])

    def stored(m, carry):
        store(m).wait()
        return carry

    lax.fori_loop(0, batches, batch, 0)
    lax.fori_loop(0, batches, stored, 0)


def coefficients(table, field, blocks, sums, ready=None):
    atoms = blocks.shape[0]
    sums[...] = jnp.zeros_like(sums)

    def batch(m, carry):
        if ready is not None:
            ready(m)
        for n in [BATCH * m + i for i in range(BATCH)]:
            entry = table[0, n]
            b = blocks[n]
            for s in range(2):
                v = field[s, pl.ds(entry & 255, WINDOW)]
                sums[s, pl.ds(entry >> 8, 1), :] = jnp.sum(jnp.sum(b * v, axis=0), axis=0, keepdims=True)
        return carry

    lax.fori_loop(0, table[1, 0], batch, 0)
    ones = jnp.ones((8, 128), jnp.float32)
    return [
        lax.dot_general(
            ones, sums[s, 0:atoms], NT, precision=lax.Precision.HIGHEST, preferred_element_type=jnp.float32
        )
        for s in range(2)
    ]


def fill_messages(y, parts, up, down):
    planes = y.shape[1]
    for s in range(2):
        up[s, 0:4] = y[s, planes - 4 : planes]
        down[s, 0:4] = y[s, 0:4]
        up[s, 4] = parts[s]
        down[s, 4] = parts[s]


def first_kernel(table, got, blocks_far, y, up, down, blocks, sums, sems):
    def load(m):
        some = pl.ds(BATCH * m, BATCH)
        return pltpu.make_async_copy(blocks_far.at[some], blocks.at[some], sems.at[m])

    def begin(m, carry):
        load(m).start()
        return carry

    lax.fori_loop(0, table[1, 0], begin, 0)
    for s in range(2):
        for j in range(got.shape[0]):
            y[s, 8 * j : 8 * j + 8] = got[j, s]
    fill_messages(y, coefficients(table, y, blocks, sums, lambda m: load(m).wait()), up, down)


def lane_weights():
    lane = lax.broadcasted_iota(jnp.int32, (8, 128), 1)
    out = []
    for k in range(1, RADIUS + 1):
        c = stencil_weights[k]
        out.append((k, jnp.where(lane >= k, c, 0.0)))
        out.append((128 - k, jnp.where(lane < 128 - k, c, 0.0)))
    return out


def row_weights():
    row = lax.broadcasted_iota(jnp.int32, (8, 128), 0)
    out = []
    for r in range(1, 8):
        near = stencil_weights[r] if r <= RADIUS else 0.0
        far = stencil_weights[8 - r] if 8 - r <= RADIUS else 0.0
        out.append((r, jnp.where(row >= r, near, far)))
    return out


def scales(mode):
    if mode == "image":
        return 1.0, 0.0
    return (1.0 if mode == "first" else 2.0) / filter_half, filter_centre


def stencil_kernel(mode, y, *refs):
    has_prev = mode == "later"
    prev, v, out, pad = refs if has_prev else (None, *refs)
    alpha, sigma = scales(mode)
    planes = y.shape[1]
    for s in range(2):
        pad[s, 0:4] = jnp.zeros((4, 8, 128), jnp.float32)
        pad[s, 4 : planes + 4] = y[s]
        pad[s, planes + 4 : planes + 8] = jnp.zeros((4, 8, 128), jnp.float32)
    half = -0.5 * alpha
    lanes = [(k, w * half) for k, w in lane_weights()]
    rows = [(k, w * half) for k, w in row_weights()]
    centre = half * 3.0 * stencil_weights[0] - alpha * sigma

    def block(j, carry):
        for s in range(2):
            line = [pad[s, 8 * j + t] for t in range(16)]
            for t in range(8):
                mid = line[t + 4]
                acc = (alpha * v[j, 2, t] + centre) * mid
                for k in range(1, RADIUS + 1):
                    acc = acc + (half * stencil_weights[k]) * (line[t + 4 + k] + line[t + 4 - k])
                for k, w in rows:
                    acc = acc + w * pltpu.roll(mid, k, 0)
                for k, w in lanes:
                    acc = acc + w * pltpu.roll(mid, k, 1)
                if has_prev:
                    acc = acc - prev[s, 8 * j + t]
                out[s, 8 * j + t] = acc
        return carry

    lax.fori_loop(0, planes // 8, block, 0)


def finish_kernel(mode, table, partial, blocks, strength, below, above, own, *refs):
    alpha, sigma = scales(mode)
    if mode == "image":
        y, send, new, splat = refs
    else:
        new, up, down, splat, sums = refs
    planes = partial.shape[1]
    atoms = blocks.shape[0]
    z = table[1, 1]
    has_low = z > 0
    has_high = z < lax.axis_size("grid") // (planes // 8) - 1
    half = -0.5 * alpha

    for s in range(2):
        total = (own[s, 4] + below[s, 4] + above[s, 4]) * strength[...] * alpha
        splat[s, 0:atoms] = jnp.transpose(jnp.broadcast_to(total[0:1], (128, 128)))
        splat[s, atoms : atoms + 8] = jnp.zeros((8, 128), jnp.float32)

    new[...] = partial[...]
    for s in range(2):
        low = [jnp.where(has_low, below[s, i], 0.0) for i in range(4)]
        high = [jnp.where(has_high, above[s, i], 0.0) for i in range(4)]
        for t in range(4):
            for side, edge in ((low, 0), (high, 1)):
                acc = None
                for k in range(t + 1, RADIUS + 1):
                    value = side[t - k + 4] if edge == 0 else side[k - t - 1]
                    term = (half * stencil_weights[k]) * value
                    acc = term if acc is None else acc + term
                p = t if edge == 0 else planes - 1 - t
                new[s, p] = new[s, p] + acc

    def spread(m, carry):
        for n in [BATCH * m + i for i in range(BATCH)]:
            entry = table[0, n]
            b = blocks[n]
            window = pl.ds(entry & 255, WINDOW)
            for s in range(2):
                c = jnp.broadcast_to(splat[s, pl.ds(entry >> 8, 1), :], (8, 128))
                new[s, window] = new[s, window] + c * b
        return carry

    lax.fori_loop(0, table[1, 0], spread, 0)

    if mode == "image":
        for s in range(2):
            for p in range(planes):
                j, t = divmod(p, 8)
                d = (t // 2) * (planes // 8) + j
                q = 8 * (t % 2)
                send[d, s, 0, q : q + 8] = y[s, p]
                send[d, s, 1, q : q + 8] = new[s, p]
    else:
        fill_messages(new, coefficients(table, new, blocks, sums), up, down)


def product_kernel(got, rows):
    states = rows.shape[0]
    total = None
    for r in range(0, 16, 2):
        f = [got[pl.ds(r + i, states, stride=32), :] for i in range(2)]
        h = [got[pl.ds(16 + r + i, states, stride=32), :] for i in range(2)]
        f = jnp.concatenate(f, axis=1)
        left = jnp.concatenate([f, jnp.concatenate(h, axis=1)], axis=0)
        term = lax.dot_general(
            left, f, NT, precision=lax.Precision.HIGHEST, preferred_element_type=jnp.float32
        )
        total = term if total is None else total + term
    rows[...] = jnp.concatenate([total[0:states], total[states : 2 * states]], axis=1)


def pack_kernel(y, parts, out):
    rows = parts[0]
    for k in range(1, parts.shape[0]):
        rows = rows + parts[k]
    for j in range(out.shape[0]):
        out[j, 0:8] = y[0, 8 * j : 8 * j + 8]
        out[j, 8:16] = y[1, 8 * j : 8 * j + 8]
        out[j, 16] = rows[0:8]
        out[j, 17] = rows[8:16]


def unpack_kernel(scale, got, filtered, gram, hamiltonian):
    width = gram.shape[1]
    for half in range(2):
        rows = got[0, 16 + half]
        for j in range(1, got.shape[0]):
            rows = rows + got[j, 16 + half]
        rows = rows * scale
        gram[8 * half : 8 * half + 8] = rows[:, 0:width]
        hamiltonian[8 * half : 8 * half + 8] = rows[:, width : 2 * width]
    for j in range(got.shape[0]):
        filtered[2 * j] = got[j, 0:8]
        filtered[2 * j + 1] = got[j, 8:16]


def per_device(states, potential, proj_index, proj_value, proj_strength):
    f32 = jnp.float32
    shape = jax.ShapeDtypeStruct
    count, depth, ny, nz = states.shape
    atoms = proj_index.shape[0]
    grid = lax.axis_size("grid")
    bands = lax.axis_size("band")
    group = 8
    zs = grid // group
    per = count // group
    planes = group * depth
    everyone = bands * count
    in_plane = [[z * group + j for j in range(group)] for z in range(zs)]
    across = [
        [b * grid + z * group + j for b in range(core, bands, 2) for z in range(zs)]
        for core in range(2)
        for j in range(group)
    ]
    whole_plane = [[b * grid + z * group + j for b in range(bands) for j in range(group)] for z in range(zs)]

    parcel = call(
        parcel_kernel,
        "parcel",
        pltpu.HBM((group, 3, depth, ny, nz), f32),
        [HBM] * 2,
        HBM,
        [
            pltpu.VMEM((group, per, depth, ny, nz), f32),
            pltpu.VMEM((depth, ny, nz), f32),
            pltpu.SemaphoreType.DMA((4, group)),
        ],
    )(far(states.reshape(group, per, depth, ny, nz)), far(potential))
    start = lax.all_to_all(parcel, "grid", 0, 0, axis_index_groups=in_plane, tiled=True)

    place = lax.axis_index("grid") // group
    support = proj_index >> 10
    low = jnp.min(support, axis=1) - place * planes
    high = jnp.max(support, axis=1) - place * planes
    entry = jnp.arange(atoms, dtype=jnp.int32) * 256 + jnp.clip(low, 0, planes - WINDOW)
    entry = jnp.where((high >= 0) & (low < planes), entry, -1)
    info = jnp.stack([entry, jnp.full((atoms,), place)]).astype(jnp.int32)

    field = shape((per, planes, ny, nz), f32)
    message = shape((per, 5, ny, nz), f32)
    sums = pltpu.VMEM((per, atoms + 8, 128), f32)
    pad = pltpu.VMEM((per, planes + 8, ny, nz), f32)
    new = pltpu.VMEM(field.shape, f32)
    strength = proj_strength.reshape(1, atoms)

    block = (atoms, WINDOW, ny, nz)
    blocks_far, table = call(
        functools.partial(build_kernel, planes),
        "build",
        (pltpu.HBM(block, f32), pltpu.SMEM((2, 256), jnp.int32)),
        [SMEM, HBM, HBM],
        (HBM, SMEM),
        [
            pltpu.VMEM(proj_index.shape, jnp.int32),
            pltpu.VMEM(proj_value.shape, f32),
            pltpu.VMEM(block, f32),
            pltpu.SemaphoreType.DMA((2 + atoms // BATCH,)),
        ],
        vmem=16,
    )(info, far(proj_index), far(proj_value))
    table = pltpu.with_memory_space_constraint(table, pltpu.SMEM)
    current, up, down, blocks = call(
        first_kernel,
        "first",
        (field, message, message, shape(block, f32)),
        [SMEM, VMEM, HBM],
        (VMEM,) * 4,
        [sums, pltpu.SemaphoreType.DMA((atoms // BATCH,))],
        vmem=16,
    )(table, start, far(blocks_far))

    def exchange(up, down):
        below = lax.ppermute(up, "grid", [(i, (i + group) % grid) for i in range(grid)])
        above = lax.ppermute(down, "grid", [(i, (i - group) % grid) for i in range(grid)])
        return below, above

    def local(mode, *arrays):
        return call(
            functools.partial(stencil_kernel, mode), "stencil", field, [VMEM] * len(arrays), VMEM, [pad]
        )(*arrays)

    previous = None
    for k in range(DEGREE):
        mode = "later" if k else "first"
        below, above = exchange(up, down)
        partial = local(mode, current, *([previous] if k else []), start)
        following, up, down = call(
            functools.partial(finish_kernel, mode),
            "finish",
            (field, message, message),
            [SMEM] + [VMEM] * 6,
            (VMEM,) * 3,
            [sums, sums],
        )(table, partial, blocks, strength, below, above, up)
        previous, current = current, following

    below, above = exchange(up, down)
    send = call(
        functools.partial(finish_kernel, "image"),
        "image",
        shape((bands * group, per, 2, 2 * ny, nz), f32),
        [SMEM] + [VMEM] * 7,
        VMEM,
        [new, sums],
    )(table, local("image", current, start), blocks, strength, below, above, up, current)
    got = lax.all_to_all(send, ("band", "grid"), 0, 0, axis_index_groups=whole_plane, tiled=True)
    part = call(product_kernel, "product", shape((everyone, 2 * everyone), f32), [VMEM], VMEM)(
        got.reshape(everyone * 32, nz)
    )
    band = lax.axis_index("band")
    part = part + lax.ppermute(part, "band", [(i, i ^ 1) for i in range(bands)])
    core = band % 2
    copies = jnp.concatenate(
        [
            jnp.broadcast_to(lax.dynamic_slice_in_dim(part, (2 * chip + core) * count, count, axis=0), (zs, count, nz))
            for chip in range(bands // 2)
        ],
        axis=0,
    )
    copies = lax.all_to_all(copies, ("band", "grid"), 0, 0, axis_index_groups=across, tiled=True)
    packed = call(pack_kernel, "pack", shape((group, 18, ny, nz), f32), [VMEM, VMEM], VMEM)(current, copies)
    packed = lax.all_to_all(packed, "grid", 0, 0, axis_index_groups=in_plane, tiled=True)
    square = shape((count, everyone), f32)
    return call(
        functools.partial(unpack_kernel, 1.0 / float(grid * depth * ny * nz)),
        "unpack",
        (shape(states.shape, f32), square, square),
        [VMEM],
        (VMEM,) * 3,
    )(packed)


def solution(mesh):
    in_specs = (P("band", "grid", None, None), P("grid", None, None), P(), P(), P())
    out_specs = (P("band", "grid", None, None), P("band", None), P("band", None))
    return jax.shard_map(
        per_device, mesh=mesh, in_specs=in_specs, out_specs=out_specs, check_vma=False
    )
```
